128 devices in a mesh: dp: 8 (over x_lo, z), tensor: 16 (over x_hi, y, core).
Axes of the slice: x: 4 (x_hi: 2, x_lo: 2; x = x_hi * 2 + x_lo), y: 4, z: 4, core: 2. Of those that a mesh axis runs over, the one named last changes fastest.
Arguments:
- tokens: bfloat16 [4096, 4096], P('dp', 'tensor'), may hold values from -6 to 6
- cotangent: bfloat16 [4096, 4096], P('dp', 'tensor'), may hold values from -6 to 6
- gate_weight: bfloat16 [4096, 14336], P('dp', 'tensor'), may hold values from -0.09375 to 0.09375
- up_weight: bfloat16 [4096, 14336], P('dp', 'tensor'), may hold values from -0.09375 to 0.09375
- down_weight: bfloat16 [4096, 14336], P('dp', 'tensor'), may hold values from -0.046875 to 0.046875
- gate_keep: int32 [32, 112], P('dp', 'tensor'), may hold values from 0 to 1, as said below
- up_keep: int32 [32, 112], P('dp', 'tensor'), may hold values from 0 to 1, as said below
- down_keep: int32 [32, 112], P('dp', 'tensor'), may hold values from 0 to 1, as said below
Outputs:
- grad_tokens: bfloat16 [4096, 4096], P('dp', 'tensor')
- grad_gate: bfloat16 [4096, 14336], P('dp', 'tensor')
- grad_up: bfloat16 [4096, 14336], P('dp', 'tensor')
- grad_down: bfloat16 [4096, 14336], P('dp', 'tensor')
The draws below stay inside these ranges and needn't reach their ends.
Inputs may be any that keep to these rules, and one draw needn't show every extreme that they name: `gate_keep`: 1 keeps the 128 x 128 tile of the gate projection, 0 prunes it; the kept share of each range of 7 tile columns held by one device of tensor lies between 0.25 and 0.75 in expectation and differs between ranges; any 0/1 mask is allowed, and no bound on the number of kept tiles in a device's [4, 7] block is promised. `up_keep`: as for gate_keep, for the up projection. `down_keep`: as for gate_keep, for the down projection.
All inputs are finite; a program needn't handle non-finite values.
Results may differ from the reference program's by a relative error of at most 0.018.
Values may be sent and summed in bfloat16 or wider, within the bound.
No kernel may reach another device: no remote copies, remote signals or barrier semaphores. Data moves between devices by JAX's collectives and lax.ppermute only.
A program may use at most 192 MiB of HBM per device.

```python
import jax
import jax.numpy as jnp
from jax import lax

D = 4096
FF = 14336
TOK_DEV = 512
TOKENS = 4096
N_DP = 8
N_TENSOR = 16


def keep_tiles(key):
    row_tiles = D // 128
    col_tiles = FF // 128
    rate_key, tile_key = jax.random.split(key)
    shuffled = jax.random.permutation(rate_key, N_TENSOR)
    shard_index = jnp.arange(col_tiles, dtype=jnp.int32) // (col_tiles // N_TENSOR)
    limit = 250 + 500 * shuffled[shard_index] // max(N_TENSOR - 1, 1)
    scores = jax.random.randint(tile_key, (row_tiles, col_tiles), 0, 1000)
    return (scores < limit[None, :]).astype(jnp.int32)


def draw_gate_keep(key, part):
    return keep_tiles(jax.random.fold_in(key, 11))


def draw_up_keep(key, part):
    return keep_tiles(jax.random.fold_in(key, 23))


def draw_down_keep(key, part):
    return keep_tiles(jax.random.fold_in(key, 37))


def shard_levels(rng, extent, shards, low, high):
    level, own = 1.0, jax.random.fold_in(rng, 6)
    for axis_at, shards_of in shards:
        steps = jnp.exp(jax.random.uniform(jax.random.fold_in(own, axis_at), (shards_of,), jnp.float32, low / len(shards), high / len(shards)))
        level = level * jnp.repeat(steps, extent[axis_at] // shards_of).reshape([-1 if axis == axis_at else 1 for axis in range(len(extent))])
    return level


def bell_draw(own_key, shape, scale, most, pieces=(), kind=jnp.bfloat16):
    drawn = scale * jax.random.normal(own_key, shape, jnp.float32)
    if pieces:
        drawn = drawn * shard_levels(own_key, shape, pieces, -0.22, 0.18)
    return jnp.clip(drawn, -most, most).astype(kind)


def setup_inputs(seed: int = 0) -> dict:
    key_list = jax.random.split(jax.random.key(seed), 9)
    tokens = bell_draw(key_list[0], (TOKENS, D), 1.0, 6.0, ((0, 8), (1, 16)))
    cotangent = bell_draw(key_list[1], (TOKENS, D), 1.0, 6.0, ((0, 8), (1, 16)))
    gate_weight = bell_draw(key_list[2], (D, FF), D ** -0.5, 0.09375, ((0, 8), (1, 16)))
    up_weight = bell_draw(key_list[3], (D, FF), D ** -0.5, 0.09375, ((0, 8), (1, 16)))
    down_weight = bell_draw(key_list[4], (D, FF), FF ** -0.5, 0.046875, ((0, 8), (1, 16)))
    gate_keep = draw_gate_keep(jax.random.fold_in(key_list[8], 71), 0)
    up_keep = draw_up_keep(jax.random.fold_in(key_list[8], 71), 0)
    down_keep = draw_down_keep(jax.random.fold_in(key_list[8], 71), 0)
    return {"tokens": tokens, "cotangent": cotangent, "gate_weight": gate_weight, "up_weight": up_weight, "down_weight": down_weight, "gate_keep": gate_keep, "up_keep": up_keep, "down_keep": down_keep}


def expand(tile_keep):
    row_tiles, col_tiles = tile_keep.shape
    spread = jnp.broadcast_to(tile_keep[:, None, :, None], (row_tiles, 128, col_tiles, 128))
    return spread.reshape(row_tiles * 128, col_tiles * 128)


def masked(weight, tile_keep):
    return weight * expand(tile_keep).astype(weight.dtype)


def silu_parts(gate_sum, up_sum):
    sigmoid_gate = jax.nn.sigmoid(gate_sum)
    return sigmoid_gate, (gate_sum * sigmoid_gate * up_sum).astype(jnp.bfloat16)


def backprop(gate_sum, up_sum, sigmoid_gate, hidden_grad):
    gate_grad = (hidden_grad * up_sum * sigmoid_gate * (1.0 + gate_sum * (1.0 - sigmoid_gate))).astype(jnp.bfloat16)
    up_grad = (hidden_grad * gate_sum * sigmoid_gate).astype(jnp.bfloat16)
    return gate_grad, up_grad


def dot_rows(former, latter):
    return lax.dot_general(former, latter, (((0,), (0,)), ((), ())), preferred_element_type=jnp.float32)


def dot_cols(former, latter):
    return lax.dot_general(former, latter, (((1,), (1,)), ((), ())), preferred_element_type=jnp.float32)


def rounded_add(running, fresh):
    return running + lax.optimization_barrier(fresh.astype(jnp.bfloat16)).astype(jnp.float32)


def reference(tokens, cotangent, gate_weight, up_weight, down_weight, gate_keep, up_keep, down_keep):
    gate_kept = masked(gate_weight, gate_keep)
    up_kept = masked(up_weight, up_keep)
    down_kept = masked(down_weight, down_keep)
    gate_sum = jnp.dot(tokens, gate_kept, preferred_element_type=jnp.float32)
    up_sum = jnp.dot(tokens, up_kept, preferred_element_type=jnp.float32)
    sigmoid_gate, hidden = silu_parts(gate_sum, up_sum)
    hidden_grad = jnp.dot(cotangent, down_kept, preferred_element_type=jnp.float32)
    gate_grad, up_grad = backprop(gate_sum, up_sum, sigmoid_gate, hidden_grad)

    col_width = FF // N_TENSOR

    def add_range(running, range_index):
        offset = (range_index * col_width).astype(jnp.int32)
        part_sum = dot_cols(lax.dynamic_slice_in_dim(gate_grad, offset, col_width, 1),
                            lax.dynamic_slice_in_dim(gate_kept, offset, col_width, 1))
        part_sum = part_sum + dot_cols(lax.dynamic_slice_in_dim(up_grad, offset, col_width, 1),
                                       lax.dynamic_slice_in_dim(up_kept, offset, col_width, 1))
        return rounded_add(running, part_sum), None

    input_sum = lax.scan(add_range, jnp.zeros(tokens.shape, jnp.float32),
                         jnp.arange(N_TENSOR, dtype=jnp.int32))[0]
    grad_tokens = input_sum.astype(jnp.bfloat16)

    def add_group(running, group_index):
        offset = (group_index * TOK_DEV).astype(jnp.int32)
        token_rows = lax.dynamic_slice_in_dim(tokens, offset, TOK_DEV, 0)
        cot_rows = lax.dynamic_slice_in_dim(cotangent, offset, TOK_DEV, 0)
        gate_rows = lax.dynamic_slice_in_dim(gate_grad, offset, TOK_DEV, 0)
        up_rows = lax.dynamic_slice_in_dim(up_grad, offset, TOK_DEV, 0)
        hidden_rows = lax.dynamic_slice_in_dim(hidden, offset, TOK_DEV, 0)
        first_total = rounded_add(running[0], dot_rows(token_rows, gate_rows))
        second_total = rounded_add(running[1], dot_rows(token_rows, up_rows))
        third_total = rounded_add(running[2], dot_rows(cot_rows, hidden_rows))
        return (first_total, second_total, third_total), None

    zero_grad = jnp.zeros(gate_weight.shape, jnp.float32)
    totals = lax.scan(add_group, (zero_grad, zero_grad, zero_grad),
                      jnp.arange(N_DP, dtype=jnp.int32))[0]
    grad_gate = (totals[0] * expand(gate_keep).astype(jnp.float32)).astype(jnp.bfloat16)
    grad_up = (totals[1] * expand(up_keep).astype(jnp.float32)).astype(jnp.bfloat16)
    grad_down = (totals[2] * expand(down_keep).astype(jnp.float32)).astype(jnp.bfloat16)
    return (grad_tokens, grad_gate, grad_up, grad_down)
```

```python
import jax
import jax.numpy as jnp
from jax import lax
from jax.experimental import pallas as pl
from jax.experimental.pallas import tpu as pltpu
from jax.sharding import Mesh
from jax.sharding import PartitionSpec as P


F32 = jnp.float32
BF16 = jnp.bfloat16
X = ("xl", "xh")
VMEM_LIMIT = 56 * 1024 * 1024
NT = (((1,), (1,)), ((), ()))
NN = (((1,), (0,)), ((), ()))
RANGE = 448
TOKENS = 1024


def shift(value, axis, size, step):
    name = (lambda i: i % 2 * 2 + i // 2) if axis == X else (lambda i: i)
    return lax.ppermute(value, axis, [(name(i), name((i + step) % size)) for i in range(size)])


def expand(tile_keep):
    row_tiles, col_tiles = tile_keep.shape
    spread = jnp.broadcast_to(tile_keep[:, None, :, None], (row_tiles, 128, col_tiles, 128))
    return spread.reshape(row_tiles * 128, col_tiles * 128)


def gather_four(block, axis):
    return jnp.stack([block] + [shift(block, axis, 4, -d) for d in (1, 2, 3)])


def send_four(pieces, axis):
    return [pieces[0]] + [shift(pieces[d], axis, 4, d) for d in (1, 2, 3)]


def total_of(blocks):
    return sum(b.astype(F32) for b in blocks).astype(BF16)


def turn_x(pos, xh, xl):
    return lax.rem(xh * 2 + xl + 4 - pos[0], 4)


def turn_y(pos, y):
    return lax.rem(y + 4 - pos[1], 4)


def act_specs(far_of, x_first):
    def spec(xl):
        def place(s, pos):
            z, far = far_of(s)
            turned = (turn_y(pos, z), turn_x(pos, far ^ pos[3], xl))
            return (turned[::-1] if x_first else turned) + (0, 0)

        return pl.BlockSpec((1, 1, 512, 256), place)

    return [spec(0), spec(0), spec(1), spec(1)]


def whole(shape):
    return pl.BlockSpec(shape, lambda *ids: (0,) * len(shape))


def by_z(count):
    return pl.BlockSpec((1, count, RANGE, 512), lambda s, *rest: (s, 0, 0, 0))


def call(kernel, name, steps, in_specs, outs, out_specs, scratch, flops, args):
    moved = sum(a.size * a.dtype.itemsize for a in args)
    return pl.pallas_call(
        kernel,
        name=name,
        out_shape=[jax.ShapeDtypeStruct(shape, kind) for shape, kind in outs],
        grid_spec=pltpu.PrefetchScalarGridSpec(
            num_scalar_prefetch=1,
            grid=steps,
            in_specs=in_specs,
            out_specs=out_specs,
            scratch_shapes=scratch,
        ),
        compiler_params=pltpu.CompilerParams(vmem_limit_bytes=VMEM_LIMIT),
        cost_estimate=pl.CostEstimate(flops=flops, bytes_accessed=moved, transcendentals=0),
    )(*args)


FLOPS = 2 * RANGE * TOKENS * 4096
SUMS = (RANGE, TOKENS)


def core_columns(pos):
    own = pl.ds(pl.multiple_of(pos[2] * 256, 256), 256)
    other = pl.ds(pl.multiple_of((1 - pos[2]) * 256, 256), 256)
    return own, other


def product(pos, w_ref, which, acts, half):
    own, other = core_columns(pos)
    return lax.dot_general(
        w_ref[0, which, :, own], acts[2 * half][0, 0], NT, preferred_element_type=F32
    ) + lax.dot_general(
        w_ref[0, which, :, other], acts[2 * half + 1][0, 0], NT, preferred_element_type=F32
    )


HALVES = (slice(0, 512), slice(512, 1024))


def near_sums_kernel(pos, w_ref, a0, b0, a1, b1, gate_ref, up_ref):
    first = pl.program_id(0) == 0
    for which, ref in enumerate((gate_ref, up_ref)):
        for half, cols in enumerate(HALVES):
            term = product(pos, w_ref, which, (a0, b0, a1, b1), half)

            @pl.when(first)
            def _():
                ref[:, cols] = term

            @pl.when(jnp.logical_not(first))
            def _():
                ref[:, cols] += term


def far_sums_kernel(pos, w_ref, a0, b0, a1, b1, gate_in, up_in, gate_ref, up_ref, hidden_ref):
    first = pl.program_id(0) == 0
    for which, (ref, start) in enumerate(((gate_ref, gate_in), (up_ref, up_in))):
        for half, cols in enumerate(HALVES):
            term = product(pos, w_ref, which, (a0, b0, a1, b1), half)

            @pl.when(first)
            def _():
                ref[:, cols] = start[:, cols] + term

            @pl.when(jnp.logical_not(first))
            def _():
                ref[:, cols] += term

    @pl.when(pl.program_id(0) == 3)
    def _():
        @pl.loop(0, RANGE // 16)
        def _(i):
            rows = pl.ds(i * 16, 16)
            gate, up = gate_ref[rows, :], up_ref[rows, :]
            hidden_ref[rows, :] = (gate * jax.nn.sigmoid(gate) * up).astype(BF16)


def hidden_grad_kernel(
    pos, w_ref, a0, b0, a1, b1, c0, d0, c1, d1, gate_ref, up_ref, gg_ref, ug_ref, gt_ref, ut_ref, acc
):
    first = pl.program_id(0) == 0
    for half, cols in enumerate(HALVES):
        term = product(pos, w_ref, 0, (a0, b0, a1, b1), half)
        term += product(pos, w_ref, 1, (c0, d0, c1, d1), half)

        @pl.when(first)
        def _():
            acc[:, cols] = term

        @pl.when(jnp.logical_not(first))
        def _():
            acc[:, cols] += term

    @pl.when(pl.program_id(0) == 3)
    def _():
        @pl.loop(0, RANGE // 16)
        def _(i):
            rows = pl.ds(i * 16, 16)
            gate, up, grad = gate_ref[rows, :], up_ref[rows, :], acc[rows, :]
            sig = jax.nn.sigmoid(gate)
            gg_ref[rows, :] = (grad * up * sig * (1.0 + gate * (1.0 - sig))).astype(BF16)
            ug_ref[rows, :] = (grad * gate * sig).astype(BF16)

        gt_ref[...] = gg_ref[...].T
        ut_ref[...] = ug_ref[...].T


def row_grads_kernel(grads, acts, out_ref, pos, place):
    own, other = core_columns(pos)
    for cols, (low, high) in ((own, (acts[0], acts[2])), (other, (acts[1], acts[3]))):
        term = lax.dot_general(grads[:, :512], low[0, 0], NN, preferred_element_type=F32)
        term += lax.dot_general(grads[:, 512:], high[0, 0], NN, preferred_element_type=F32)
        out_ref[0, place, :, cols] = term.astype(BF16)


def pair_grads_kernel(pos, g_ref, u_ref, a0, b0, a1, b1, out_ref):
    row_grads_kernel(g_ref, (a0, b0, a1, b1), out_ref, pos, 0)
    row_grads_kernel(u_ref, (a0, b0, a1, b1), out_ref, pos, 1)


def down_grads_kernel(pos, h_ref, a0, b0, a1, b1, c0, d0, c1, d1, out_ref):
    row_grads_kernel(h_ref, (a0, b0, a1, b1), out_ref, pos, 0)
    row_grads_kernel(h_ref, (c0, d0, c1, d1), out_ref, pos, 1)


def token_grads_kernel(pos, g_ref, u_ref, near_ref, far_ref, out_ref):
    own, other = core_columns(pos)
    for far, w_ref in ((0, near_ref), (1, far_ref)):

        @pl.when(pl.program_id(1) == far)
        def _():
            for place, cols in ((0, own), (1, other)):
                term = lax.dot_general(g_ref[...], w_ref[0, 0, :, cols], NN, preferred_element_type=F32)
                term += lax.dot_general(u_ref[...], w_ref[0, 1, :, cols], NN, preferred_element_type=F32)
                out_ref[place, 0, 0] = term.astype(BF16)


def token_grads(pos, gate_t, up_t, near, far_w):
    def place(z, far, xl, pos):
        return (0, turn_y(pos, z), turn_x(pos, far ^ pos[3], xl), 0, 0)

    half = pl.BlockSpec((512, RANGE), lambda z, far, xl, pos: (xl, 0))
    return call(
        token_grads_kernel,
        "token_grads",
        (4, 2, 2),
        [half, half, by_z(2), by_z(2)],
        [((2, 4, 4, 512, 256), BF16)],
        [pl.BlockSpec((2, 1, 1, 512, 256), place)],
        [],
        2 * FLOPS,
        (pos, gate_t, up_t, near, far_w),
    )[0]


def on_device(
    tokens, cotangent, gate_weight, up_weight, down_weight, gate_keep, up_keep, down_keep
):
    xl = lax.axis_index("xl")
    place_x = lax.axis_index("xh") * 2 + xl
    pos = jnp.stack([place_x, lax.axis_index("y"), lax.axis_index("c"), xl]).astype(jnp.int32)
    barrier = lax.optimization_barrier

    def ranges(weight, tile_keep):
        kept = (weight * expand(tile_keep).astype(BF16)).T.reshape(2, RANGE, 512)
        return (
            lax.dynamic_index_in_dim(kept, xl, 0, keepdims=False),
            lax.dynamic_index_in_dim(kept, 1 - xl, 0, keepdims=False),
        )

    gate_own, gate_other = ranges(gate_weight, gate_keep)
    up_own, up_other = ranges(up_weight, up_keep)
    down_own, down_other = ranges(down_weight, down_keep)

    def over_z(first, second):
        return lax.all_gather(jnp.stack([first, second])[None], "z", axis=0, tiled=True)

    def over_z_sum(rows):
        return lax.psum_scatter(rows, "z", scatter_dimension=0, tiled=True)[0]

    near = over_z(gate_own, up_own)
    gate_far = shift(gate_other, "xl", 2, 1)
    up_far = shift(up_other, "xl", 2, 1)
    down_far = shift(down_other, "xl", 2, 1)
    far = over_z(gate_far, up_far)
    down_full = over_z(down_own, down_far)

    tokens_x = gather_four(tokens, X)
    cot_y = gather_four(cotangent, "y")
    tokens_x, cot_y, _, _, _ = barrier((tokens_x, cot_y, gate_far, up_far, down_far))
    tokens_own = gather_four(tokens_x, "y")
    cot_own = gather_four(cot_y, X)
    tokens_swap = shift(tokens_own, "c", 2, 1)
    cot_swap = shift(cot_own, "c", 2, 1)
    token_args = (tokens_own, tokens_swap, tokens_own, tokens_swap)
    cot_args = (cot_own, cot_swap, cot_own, cot_swap)

    def near_rows(s):
        return s, 0

    def far_rows(s):
        return s, 1

    gate_near, up_near = call(
        near_sums_kernel,
        "near_sums",
        (4,),
        [by_z(2)] + act_specs(near_rows, False),
        [(SUMS, F32), (SUMS, F32)],
        [whole(SUMS), whole(SUMS)],
        [],
        FLOPS,
        (pos, near) + token_args,
    )
    gate_sum, up_sum, hidden = call(
        far_sums_kernel,
        "far_sums",
        (4,),
        [by_z(2)] + act_specs(far_rows, False) + [whole(SUMS)] * 2,
        [(SUMS, F32), (SUMS, F32), (SUMS, BF16)],
        [whole(SUMS)] * 3,
        [],
        FLOPS,
        (pos, far) + token_args + (gate_near, up_near),
    )
    (down_rows,) = call(
        down_grads_kernel,
        "down_grads",
        (4,),
        [whole(SUMS)] + act_specs(near_rows, True) + act_specs(far_rows, True),
        [((4, 2, RANGE, 512), BF16)],
        [by_z(2)],
        [],
        FLOPS,
        (pos, hidden) + cot_args + cot_args,
    )
    gate_grad, up_grad, gate_t, up_t = call(
        hidden_grad_kernel,
        "hidden_grad",
        (4,),
        [by_z(2)] + act_specs(near_rows, True) + act_specs(far_rows, True) + [whole(SUMS)] * 2,
        [(SUMS, BF16), (SUMS, BF16), (SUMS[::-1], BF16), (SUMS[::-1], BF16)],
        [whole(SUMS), whole(SUMS), whole(SUMS[::-1]), whole(SUMS[::-1])],
        [pltpu.VMEM(SUMS, F32)],
        FLOPS,
        (pos, down_full) + cot_args + cot_args + (gate_sum, up_sum),
    )

    def pair_rows(name, rows_of):
        return call(
            pair_grads_kernel,
            name,
            (4,),
            [whole(SUMS)] * 2 + act_specs(rows_of, False),
            [((4, 2, RANGE, 512), BF16)],
            [by_z(2)],
            [],
            FLOPS,
            (pos, gate_grad, up_grad) + token_args,
        )[0]

    far_grads = pair_rows("far_grads", far_rows)
    near_grads = pair_rows("near_grads", near_rows)

    down_sum = over_z_sum(down_rows)
    far_sum = over_z_sum(far_grads)
    near_sum = over_z_sum(near_grads)

    parts = token_grads(pos, gate_t, up_t, near, far)
    of_chip = total_of((parts[0], shift(parts[1], "c", 2, 1)))
    of_chip, down_sum = barrier((of_chip, down_sum))
    down_back = shift(down_sum[1], "xl", 2, 1)
    beside = [shift(of_chip[1], "y", 4, 1), shift(of_chip[3], "y", 4, 3)]
    of_chip, beside, down_back, far_sum = barrier((of_chip, beside, down_back, far_sum))
    gate_back = shift(far_sum[0], "xl", 2, 1)
    up_back = shift(far_sum[1], "xl", 2, 1)
    along_y = total_of([of_chip[0], beside[0], shift(of_chip[2], "y", 4, 2), beside[1]])
    along_y, gate_back, up_back = barrier((along_y, gate_back, up_back))
    grad_tokens = total_of(send_four(along_y, X))
    grad_tokens, near_sum = barrier((grad_tokens, near_sum))

    def own_rows(own, other, tile_keep):
        both = jnp.where(xl == 0, jnp.stack([own, other]), jnp.stack([other, own]))
        grad = both.reshape(2 * RANGE, 512).T
        return (grad.astype(F32) * expand(tile_keep).astype(F32)).astype(BF16)

    grad_down = own_rows(down_sum[0], down_back, down_keep)
    grad_gate = own_rows(near_sum[0], gate_back, gate_keep)
    grad_up = own_rows(near_sum[1], up_back, up_keep)
    return (grad_tokens, grad_gate, grad_up, grad_down)


def solution(mesh):
    fine = Mesh(mesh.devices.reshape(2, 4, 2, 4, 2), ("xl", "z", "xh", "y", "c"))
    spec = P(("xl", "z"), ("xh", "y", "c"))
    return jax.shard_map(
        on_device, mesh=fine, in_specs=(spec,) * 8, out_specs=(spec,) * 4, check_vma=False
    )
```

```python
import jax
import jax.numpy as jnp
from jax import lax
from jax.experimental import pallas as pl
from jax.experimental.pallas import tpu as pltpu
from jax.sharding import Mesh
from jax.sharding import PartitionSpec as P


F32 = jnp.float32
BF16 = jnp.bfloat16
X = ("xl", "xh")
VMEM_LIMIT = 56 * 1024 * 1024
NT = (((1,), (1,)), ((), ()))
NN = (((1,), (0,)), ((), ()))
RANGE = 448
TOKENS = 1024


def shift(value, axis, size, step):
    name = (lambda i: i % 2 * 2 + i // 2) if axis == X else (lambda i: i)
    return lax.ppermute(value, axis, [(name(i), name((i + step) % size)) for i in range(size)])


def expand(tile_keep):
    row_tiles, col_tiles = tile_keep.shape
    spread = jnp.broadcast_to(tile_keep[:, None, :, None], (row_tiles, 128, col_tiles, 128))
    return spread.reshape(row_tiles * 128, col_tiles * 128)


def gather_four(block, axis):
    return jnp.stack([block] + [shift(block, axis, 4, -d) for d in (1, 2, 3)])


def send_four(pieces, axis):
    return [pieces[0]] + [shift(pieces[d], axis, 4, d) for d in (1, 2, 3)]


def ring_gather(block):
    left, right = shift(block, "z", 4, 1), shift(block, "z", 4, -1)
    cut = (2, block.shape[0] * block.shape[1] // 2, block.shape[2])
    across = jnp.stack(
        [shift(left.reshape(cut)[0], "z", 4, 1), shift(right.reshape(cut)[1], "z", 4, -1)]
    )
    return jnp.stack([block, right, across.reshape(block.shape), left])


def ring_scatter(pieces):
    own, right, across, left = (pieces[d] for d in range(4))
    low, high = shift(across[0], "z", 4, 1), shift(across[1], "z", 4, -1)
    right_0, right_1, left_0, left_1 = right[0], right[1], left[0], left[1]
    right_0, left_1 = total_of((right_0, low)), total_of((left_1, high))
    to_right, to_left = jnp.stack([right_0, right_1]), jnp.stack([left_0, left_1])
    return [own, shift(to_right, "z", 4, 1), shift(to_left, "z", 4, -1)]


def total_of(blocks):
    return sum(b.astype(F32) for b in blocks).astype(BF16)


def turn_x(pos, xh, xl):
    return lax.rem(xh * 2 + xl + 4 - pos[0], 4)


def turn_y(pos, y):
    return lax.rem(y + 4 - pos[1], 4)


def act_specs(far_of, x_first):
    def spec(xl):
        def place(s, pos):
            z, far = far_of(s)
            turned = (turn_y(pos, z), turn_x(pos, far ^ pos[3], xl))
            return (turned[::-1] if x_first else turned) + (0, 0)

        return pl.BlockSpec((1, 1, 512, 256), place)

    return [spec(0), spec(0), spec(1), spec(1)]


def whole(shape):
    return pl.BlockSpec(shape, lambda *ids: (0,) * len(shape))


def by_z(count, first):
    return pl.BlockSpec((1, count, RANGE, 512), lambda s, *rest: (s, first, 0, 0))


def by_turned_z(count, first):
    def place(s, *rest):
        return (lax.rem(s + 4 - rest[-1][4], 4), first, 0, 0)

    return pl.BlockSpec((1, count, RANGE, 512), place)


def call(kernel, steps, in_specs, outs, out_specs, scratch, flops, args):
    moved = sum(a.size * a.dtype.itemsize for a in args)
    return pl.pallas_call(
        kernel,
        out_shape=[jax.ShapeDtypeStruct(shape, kind) for shape, kind in outs],
        grid_spec=pltpu.PrefetchScalarGridSpec(
            num_scalar_prefetch=1,
            grid=steps,
            in_specs=in_specs,
            out_specs=out_specs,
            scratch_shapes=scratch,
        ),
        compiler_params=pltpu.CompilerParams(vmem_limit_bytes=VMEM_LIMIT),
        cost_estimate=pl.CostEstimate(flops=flops, bytes_accessed=moved, transcendentals=0),
    )(*args)


FLOPS = 2 * RANGE * TOKENS * 4096
SUMS = (RANGE, TOKENS)
PAIR = (2 * RANGE, TOKENS)


def core_columns(pos):
    own = pl.ds(pl.multiple_of(pos[2] * 256, 256), 256)
    other = pl.ds(pl.multiple_of((1 - pos[2]) * 256, 256), 256)
    return own, other


def own_first(pos, w):
    own, other = core_columns(pos)
    return jnp.concatenate([w[:, own], w[:, other]], axis=1)


def beside(own_ref, other_ref):
    return jnp.concatenate([own_ref[0, 0], other_ref[0, 0]], axis=1)


HALVES = (slice(0, 512), slice(512, 1024))


def near_sums_kernel(pos, w_ref, a0, b0, a1, b1, sums_ref):
    first = pl.program_id(0) == 0
    w = own_first(pos, w_ref.at[0].reshape(2 * RANGE, 512))
    for cols, (own, other) in zip(HALVES, ((a0, b0), (a1, b1))):
        term = lax.dot_general(w, beside(own, other), NT, preferred_element_type=F32)

        @pl.when(first)
        def _():
            sums_ref[:, cols] = term

        @pl.when(jnp.logical_not(first))
        def _():
            sums_ref[:, cols] += term


def far_sums_kernel(pos, w_ref, a0, b0, a1, b1, near_ref, sums_ref, hidden_ref):
    first = pl.program_id(0) == 0
    w = own_first(pos, w_ref.at[0].reshape(2 * RANGE, 512))
    for cols, (own, other) in zip(HALVES, ((a0, b0), (a1, b1))):
        term = lax.dot_general(w, beside(own, other), NT, preferred_element_type=F32)

        @pl.when(first)
        def _():
            sums_ref[:, cols] = near_ref[:, cols] + term

        @pl.when(jnp.logical_not(first))
        def _():
            sums_ref[:, cols] += term

    @pl.when(pl.program_id(0) == 3)
    def _():
        @pl.loop(0, RANGE // 16)
        def _(i):
            gate = sums_ref[pl.ds(i * 16, 16), :]
            up = sums_ref[pl.ds(RANGE + i * 16, 16), :]
            hidden_ref[pl.ds(i * 16, 16), :] = (gate * jax.nn.sigmoid(gate) * up).astype(BF16)


def hidden_grad_kernel(
    pos, near_ref, far_ref, a0, b0, a1, b1, c0, d0, c1, d1, sums_ref, grads_ref, turned_ref, acc
):
    first = pl.program_id(0) == 0
    near, far = own_first(pos, near_ref.at[0, 0]), own_first(pos, far_ref.at[0, 0])
    for cols, pairs in zip(HALVES, ((a0, b0, c0, d0), (a1, b1, c1, d1))):
        term = lax.dot_general(near, beside(*pairs[:2]), NT, preferred_element_type=F32)
        term += lax.dot_general(far, beside(*pairs[2:]), NT, preferred_element_type=F32)

        @pl.when(first)
        def _():
            acc[:, cols] = term

        @pl.when(jnp.logical_not(first))
        def _():
            acc[:, cols] += term

    @pl.when(pl.program_id(0) == 3)
    def _():
        @pl.loop(0, RANGE // 16)
        def _(i):
            gates, ups = pl.ds(i * 16, 16), pl.ds(RANGE + i * 16, 16)
            gate, up, grad = sums_ref[gates, :], sums_ref[ups, :], acc[gates, :]
            sig = jax.nn.sigmoid(gate)
            grads_ref[gates, :] = (grad * up * sig * (1.0 + gate * (1.0 - sig))).astype(BF16)
            grads_ref[ups, :] = (grad * gate * sig).astype(BF16)

        @pl.loop(0, TOKENS // 128)
        def _(i):
            part = pl.ds(pl.multiple_of(i * 128, 128), 128)
            turned_ref[part, :] = grads_ref[:, part].T


def pair_grads_kernel(pos, g_ref, a0, b0, a1, b1, out_ref):
    own, other = core_columns(pos)
    for cols, low, high in ((own, a0, a1), (other, b0, b1)):
        acts = jnp.concatenate([low[0, 0], high[0, 0]], axis=0)
        term = lax.dot_general(g_ref[...], acts, NN, preferred_element_type=F32).astype(BF16)
        out_ref[0, 0, :, cols] = term[:RANGE]
        out_ref[0, 1, :, cols] = term[RANGE:]


def down_grads_kernel(pos, h_ref, a0, b0, a1, b1, c0, d0, c1, d1, out_ref):
    own, other = core_columns(pos)
    for place, cols, low, high in ((0, own, a0, a1), (0, other, b0, b1), (1, own, c0, c1), (1, other, d0, d1)):
        acts = jnp.concatenate([low[0, 0], high[0, 0]], axis=0)
        term = lax.dot_general(h_ref[...], acts, NN, preferred_element_type=F32)
        out_ref[0, place, :, cols] = term.astype(BF16)


def token_grads_kernel(pos, g_ref, near_ref, far_ref, out_ref):
    here, far = pos[2], pl.program_id(1)
    near_w, far_w = (ref.at[0].reshape(2 * RANGE, 512)[...] for ref in (near_ref, far_ref))
    w = jnp.where(far == 0, near_w, far_w)
    term = lax.dot_general(g_ref[...], w, NN, preferred_element_type=F32).astype(BF16)
    for xl in (0, 1):
        place = turn_x(pos, far ^ pos[3], xl)
        out_ref[here, 0, place] = term[xl * 512 : (xl + 1) * 512, :256]
        out_ref[1 - here, 0, place] = term[xl * 512 : (xl + 1) * 512, 256:]


def token_grads(pos, turned, near, far_w):
    def place(z, far, pos):
        return (0, turn_y(pos, z), 0, 0, 0)

    return call(
        token_grads_kernel,
        (4, 2),
        [whole(turned.shape), by_z(2, 0), by_turned_z(2, 0)],
        [((2, 4, 4, 512, 256), BF16)],
        [pl.BlockSpec((2, 1, 4, 512, 256), place)],
        [],
        2 * FLOPS,
        (pos, turned, near, far_w),
    )[0]


def on_device(
    tokens, cotangent, gate_weight, up_weight, down_weight, gate_keep, up_keep, down_keep
):
    xl = lax.axis_index("xl")
    place_x = lax.axis_index("xh") * 2 + xl
    pos = jnp.stack(
        [place_x, lax.axis_index("y"), lax.axis_index("c"), xl, lax.axis_index("z")]
    ).astype(jnp.int32)
    barrier = lax.optimization_barrier

    def ranges(weight, tile_keep):
        kept = (weight * expand(tile_keep).astype(BF16)).T.reshape(2, RANGE, 512)
        return (
            lax.dynamic_index_in_dim(kept, xl, 0, keepdims=False),
            lax.dynamic_index_in_dim(kept, 1 - xl, 0, keepdims=False),
        )

    gate_own, gate_other = ranges(gate_weight, gate_keep)
    up_own, up_other = ranges(up_weight, up_keep)
    down_own, down_other = ranges(down_weight, down_keep)

    def over_z_sum(rows):
        return lax.psum_scatter(rows, "z", scatter_dimension=0, tiled=True)[0]

    near = lax.all_gather(jnp.stack([gate_own, up_own, down_own])[None], "z", axis=0, tiled=True)
    tokens_x = gather_four(tokens, X)
    cot_y = gather_four(cotangent, "y")
    others = jnp.stack([gate_other, up_other, down_other])
    tokens_x, cot_y, others = barrier((tokens_x, cot_y, others))
    far_here = shift(others, "xl", 2, 1)
    tokens_up, tokens_low = shift(tokens_x, "y", 4, -1), shift(tokens_x, "y", 4, 1)
    tokens_across = shift(tokens_x, "y", 4, 2)
    cot_y, far_here = barrier((cot_y, far_here))
    far = ring_gather(far_here)
    cot_own = [cot_y] + [shift(cot_y, X, 4, -d) for d in (1, 2, 3)]
    cot_own = jnp.stack(cot_own)
    tokens_own = jnp.stack([tokens_x, tokens_up, tokens_across, tokens_low])
    tokens_swap = shift(tokens_own, "c", 2, 1)
    cot_swap = shift(cot_own, "c", 2, 1)
    token_args = (tokens_own, tokens_swap, tokens_own, tokens_swap)
    cot_args = (cot_own, cot_swap, cot_own, cot_swap)

    def near_rows(s):
        return s, 0

    def far_rows(s):
        return s, 1

    rows_shape = (4, 2, RANGE, 512)
    (near_sums,) = call(
        near_sums_kernel,
        (4,),
        [by_z(2, 0)] + act_specs(near_rows, False),
        [(PAIR, F32)],
        [whole(PAIR)],
        [],
        FLOPS,
        (pos, near) + token_args,
    )
    sums, hidden = call(
        far_sums_kernel,
        (4,),
        [by_turned_z(2, 0)] + act_specs(far_rows, False) + [whole(PAIR)],
        [(PAIR, F32), (SUMS, BF16)],
        [whole(PAIR), whole(SUMS)],
        [],
        FLOPS,
        (pos, far) + token_args + (near_sums,),
    )
    (down_rows,) = call(
        down_grads_kernel,
        (4,),
        [whole(SUMS)] + act_specs(near_rows, True) + act_specs(far_rows, True),
        [(rows_shape, BF16)],
        [by_z(2, 0)],
        [],
        FLOPS,
        (pos, hidden) + cot_args + cot_args,
    )
    down_rows, sums = barrier((down_rows, sums))
    down_sum = over_z_sum(down_rows)
    grads, turned = call(
        hidden_grad_kernel,
        (4,),
        [by_z(1, 2), by_turned_z(1, 2)] + act_specs(near_rows, True) + act_specs(far_rows, True) + [whole(PAIR)],
        [(PAIR, BF16), (PAIR[::-1], BF16)],
        [whole(PAIR), whole(PAIR[::-1])],
        [pltpu.VMEM(SUMS, F32)],
        FLOPS,
        (pos, near, far) + cot_args + cot_args + (sums,),
    )

    def pair_rows(rows_of, out_spec, grads):
        return call(
            pair_grads_kernel,
            (4,),
            [whole(PAIR)] + act_specs(rows_of, False),
            [(rows_shape, BF16)],
            [out_spec],
            [],
            FLOPS,
            (pos, grads) + token_args,
        )[0]

    parts = token_grads(pos, turned, near, far)
    parts, grads = barrier((parts, grads))
    core_part = shift(parts[1], "c", 2, 1)
    far_grads = pair_rows(far_rows, by_turned_z(2, 0), grads)
    far_blocks = ring_scatter(far_grads)
    far_grads, grads = barrier((far_grads, grads))
    near_grads = pair_rows(near_rows, by_z(2, 0), grads)
    near_sum = over_z_sum(near_grads)
    of_chip = total_of((parts[0], core_part))
    y_blocks = send_four(of_chip, "y")
    down_back = shift(down_sum[1], "xl", 2, 1)
    far_row = total_of(far_blocks)
    far_back = shift(far_row, "xl", 2, 1)
    y_blocks, down_back = barrier((y_blocks, down_back))
    along_y = total_of(y_blocks)
    grad_tokens = total_of(send_four(along_y, X))
    grad_tokens, near_sum, far_back = barrier((grad_tokens, near_sum, far_back))
    gate_back, up_back = far_back[0], far_back[1]

    def own_rows(own, other, tile_keep):
        both = jnp.where(xl == 0, jnp.stack([own, other]), jnp.stack([other, own]))
        grad = both.reshape(2 * RANGE, 512).T
        return (grad.astype(F32) * expand(tile_keep).astype(F32)).astype(BF16)

    grad_down = own_rows(down_sum[0], down_back, down_keep)
    grad_gate = own_rows(near_sum[0], gate_back, gate_keep)
    grad_up = own_rows(near_sum[1], up_back, up_keep)
    return (grad_tokens, grad_gate, grad_up, grad_down)


def solution(mesh):
    fine = Mesh(mesh.devices.reshape(2, 4, 2, 4, 2), ("xl", "z", "xh", "y", "c"))
    spec = P(("xl", "z"), ("xh", "y", "c"))

    return jax.shard_map(
        on_device, mesh=fine, in_specs=(spec,) * 8, out_specs=(spec,) * 4, check_vma=False
    )
```

```python
import jax
import jax.numpy as jnp
from jax import lax
from jax.experimental import pallas as pl
from jax.experimental.pallas import tpu as pltpu
from jax.sharding import Mesh
from jax.sharding import PartitionSpec as P


F32 = jnp.float32
BF16 = jnp.bfloat16
X = ("xl", "xh")
VMEM_LIMIT = 56 * 1024 * 1024
NT = (((1,), (1,)), ((), ()))
NN = (((1,), (0,)), ((), ()))
RANGE = 448
TOKENS = 1024


def shift(value, axis, size, step):
    name = (lambda i: i % 2 * 2 + i // 2) if axis == X else (lambda i: i)
    return lax.ppermute(value, axis, [(name(i), name((i + step) % size)) for i in range(size)])


def expand(tile_keep):
    row_tiles, col_tiles = tile_keep.shape
    spread = jnp.broadcast_to(tile_keep[:, None, :, None], (row_tiles, 128, col_tiles, 128))
    return spread.reshape(row_tiles * 128, col_tiles * 128)


def gather_four(block, axis):
    return jnp.stack([block] + [shift(block, axis, 4, -d) for d in (1, 2, 3)])


def send_four(pieces, axis):
    return [pieces[0]] + [shift(pieces[d], axis, 4, d) for d in (1, 2, 3)]


def ring_gather(block):
    left, right = shift(block, "z", 4, 1), shift(block, "z", 4, -1)
    cut = (2, block.shape[0] * block.shape[1] // 2, block.shape[2])
    across = jnp.stack(
        [shift(left.reshape(cut)[0], "z", 4, 1), shift(right.reshape(cut)[1], "z", 4, -1)]
    )
    return jnp.stack([block, right, across.reshape(block.shape), left])


def total_of(blocks):
    return sum(b.astype(F32) for b in blocks).astype(BF16)


def turn_x(pos, xh, xl):
    return lax.rem(xh * 2 + xl + 4 - pos[0], 4)


def turn_y(pos, y):
    return lax.rem(y + 4 - pos[1], 4)


def act_specs(far_of, x_first):
    def spec(xl):
        def place(s, pos):
            z, far = far_of(s)
            turned = (turn_y(pos, z), turn_x(pos, far ^ pos[3], xl))
            return (turned[::-1] if x_first else turned) + (0, 0)

        return pl.BlockSpec((1, 1, 512, 256), place)

    return [spec(0), spec(0), spec(1), spec(1)]


def whole(shape):
    return pl.BlockSpec(shape, lambda *ids: (0,) * len(shape))


def by_z(count, first):
    return pl.BlockSpec((1, count, RANGE, 512), lambda s, *rest: (s, first, 0, 0))


def by_turned_z(count, first):
    def place(s, *rest):
        return (lax.rem(s + 4 - rest[-1][4], 4), first, 0, 0)

    return pl.BlockSpec((1, count, RANGE, 512), place)


def call(kernel, steps, in_specs, outs, out_specs, scratch, flops, args):
    moved = sum(a.size * a.dtype.itemsize for a in args)
    return pl.pallas_call(
        kernel,
        out_shape=[jax.ShapeDtypeStruct(shape, kind) for shape, kind in outs],
        grid_spec=pltpu.PrefetchScalarGridSpec(
            num_scalar_prefetch=1,
            grid=steps,
            in_specs=in_specs,
            out_specs=out_specs,
            scratch_shapes=scratch,
        ),
        compiler_params=pltpu.CompilerParams(vmem_limit_bytes=VMEM_LIMIT),
        cost_estimate=pl.CostEstimate(flops=flops, bytes_accessed=moved, transcendentals=0),
    )(*args)


FLOPS = 2 * RANGE * TOKENS * 4096
SUMS = (RANGE, TOKENS)
PAIR = (2 * RANGE, TOKENS)


def core_columns(pos):
    own = pl.ds(pl.multiple_of(pos[2] * 256, 256), 256)
    other = pl.ds(pl.multiple_of((1 - pos[2]) * 256, 256), 256)
    return own, other


def own_first(pos, w):
    own, other = core_columns(pos)
    return jnp.concatenate([w[:, own], w[:, other]], axis=1)


def beside(own_ref, other_ref):
    return jnp.concatenate([own_ref[0, 0], other_ref[0, 0]], axis=1)


HALVES = (slice(0, 512), slice(512, 1024))


def near_sums_kernel(pos, w_ref, a0, b0, a1, b1, sums_ref):
    first = pl.program_id(0) == 0
    w = own_first(pos, w_ref.at[0].reshape(2 * RANGE, 512))
    for cols, (own, other) in zip(HALVES, ((a0, b0), (a1, b1))):
        term = lax.dot_general(w, beside(own, other), NT, preferred_element_type=F32)

        @pl.when(first)
        def _():
            sums_ref[:, cols] = term

        @pl.when(jnp.logical_not(first))
        def _():
            sums_ref[:, cols] += term


def far_sums_kernel(pos, w_ref, a0, b0, a1, b1, near_ref, sums_ref, hidden_ref):
    first = pl.program_id(0) == 0
    w = own_first(pos, w_ref.at[0].reshape(2 * RANGE, 512))
    for cols, (own, other) in zip(HALVES, ((a0, b0), (a1, b1))):
        term = lax.dot_general(w, beside(own, other), NT, preferred_element_type=F32)

        @pl.when(first)
        def _():
            sums_ref[:, cols] = near_ref[:, cols] + term

        @pl.when(jnp.logical_not(first))
        def _():
            sums_ref[:, cols] += term

    @pl.when(pl.program_id(0) == 3)
    def _():
        @pl.loop(0, RANGE // 16)
        def _(i):
            gate = sums_ref[pl.ds(i * 16, 16), :]
            up = sums_ref[pl.ds(RANGE + i * 16, 16), :]
            hidden_ref[pl.ds(i * 16, 16), :] = (gate * jax.nn.sigmoid(gate) * up).astype(BF16)


def hidden_grad_kernel(
    pos, near_ref, far_ref, a0, b0, a1, b1, c0, d0, c1, d1, sums_ref, grads_ref, turned_ref, acc
):
    first = pl.program_id(0) == 0
    near, far = own_first(pos, near_ref.at[0, 0]), own_first(pos, far_ref.at[0, 0])
    for cols, pairs in zip(HALVES, ((a0, b0, c0, d0), (a1, b1, c1, d1))):
        term = lax.dot_general(near, beside(*pairs[:2]), NT, preferred_element_type=F32)
        term += lax.dot_general(far, beside(*pairs[2:]), NT, preferred_element_type=F32)

        @pl.when(first)
        def _():
            acc[:, cols] = term

        @pl.when(jnp.logical_not(first))
        def _():
            acc[:, cols] += term

    @pl.when(pl.program_id(0) == 3)
    def _():
        @pl.loop(0, RANGE // 16)
        def _(i):
            gates, ups = pl.ds(i * 16, 16), pl.ds(RANGE + i * 16, 16)
            gate, up, grad = sums_ref[gates, :], sums_ref[ups, :], acc[gates, :]
            sig = jax.nn.sigmoid(gate)
            grads_ref[gates, :] = (grad * up * sig * (1.0 + gate * (1.0 - sig))).astype(BF16)
            grads_ref[ups, :] = (grad * gate * sig).astype(BF16)

        @pl.loop(0, TOKENS // 128)
        def _(i):
            part = pl.ds(pl.multiple_of(i * 128, 128), 128)
            turned_ref[part, :] = grads_ref[:, part].T


def pair_grads_kernel(pos, g_ref, a0, b0, a1, b1, out_ref):
    own, other = core_columns(pos)
    for cols, low, high in ((own, a0, a1), (other, b0, b1)):
        acts = jnp.concatenate([low[0, 0], high[0, 0]], axis=0)
        term = lax.dot_general(g_ref[...], acts, NN, preferred_element_type=F32).astype(BF16)
        out_ref[0, 0, :, cols] = term[:RANGE]
        out_ref[0, 1, :, cols] = term[RANGE:]


def down_grads_kernel(pos, h_ref, a0, b0, a1, b1, c0, d0, c1, d1, out_ref):
    own, other = core_columns(pos)
    for place, cols, low, high in ((0, own, a0, a1), (0, other, b0, b1), (1, own, c0, c1), (1, other, d0, d1)):
        acts = jnp.concatenate([low[0, 0], high[0, 0]], axis=0)
        term = lax.dot_general(h_ref[...], acts, NN, preferred_element_type=F32)
        out_ref[0, place, :, cols] = term.astype(BF16)


def token_grads_kernel(pos, g_ref, near_ref, far_ref, out_ref):
    here, far = pos[2], pl.program_id(1)
    near_w, far_w = (ref.at[0].reshape(2 * RANGE, 512)[...] for ref in (near_ref, far_ref))
    w = jnp.where(far == 0, near_w, far_w)
    term = lax.dot_general(g_ref[...], w, NN, preferred_element_type=F32).astype(BF16)
    for xl in (0, 1):
        place = turn_x(pos, far ^ pos[3], xl)
        out_ref[here, 0, place] = term[xl * 512 : (xl + 1) * 512, :256]
        out_ref[1 - here, 0, place] = term[xl * 512 : (xl + 1) * 512, 256:]


def token_grads(pos, turned, near, far_w):
    def place(z, far, pos):
        return (0, turn_y(pos, z), 0, 0, 0)

    return call(
        token_grads_kernel,
        (4, 2),
        [whole(turned.shape), by_z(2, 0), by_z(2, 0)],
        [((2, 4, 4, 512, 256), BF16)],
        [pl.BlockSpec((2, 1, 4, 512, 256), place)],
        [],
        2 * FLOPS,
        (pos, turned, near, far_w),
    )[0]


def on_device(
    tokens, cotangent, gate_weight, up_weight, down_weight, gate_keep, up_keep, down_keep
):
    xl = lax.axis_index("xl")
    place_x = lax.axis_index("xh") * 2 + xl
    pos = jnp.stack(
        [place_x, lax.axis_index("y"), lax.axis_index("c"), xl, lax.axis_index("z")]
    ).astype(jnp.int32)
    barrier = lax.optimization_barrier
    one = (pos[4] < 4).astype(BF16)

    def ranges(weight, tile_keep):
        kept = (weight * expand(tile_keep).astype(BF16)).T.reshape(2, RANGE, 512)
        return (
            lax.dynamic_index_in_dim(kept, xl, 0, keepdims=False),
            lax.dynamic_index_in_dim(kept, 1 - xl, 0, keepdims=False),
        )

    gate_own, gate_other = ranges(gate_weight, gate_keep)
    up_own, up_other = ranges(up_weight, up_keep)
    down_own, down_other = ranges(down_weight, down_keep)

    def over_z_sum(rows):
        return lax.psum_scatter(rows, "z", scatter_dimension=0, tiled=True)[0]

    def over_z(rows):
        return lax.all_gather(rows[None], "z", axis=0, tiled=True)

    near = over_z(jnp.stack([gate_own, up_own]))
    tokens_x = gather_four(tokens, X)
    cot_y = gather_four(cotangent, "y")
    tokens_x, cot_y, gate_other, up_other, down_other = barrier(
        (tokens_x, cot_y, gate_other, up_other, down_other)
    )
    gate_far, up_far = shift(gate_other, "xl", 2, 1), shift(up_other, "xl", 2, 1)
    down_far = shift(down_other, "xl", 2, 1)
    far_here = jnp.stack([gate_far, up_far])
    far = over_z(far_here)
    tokens_up, tokens_low = shift(tokens_x, "y", 4, -1), shift(tokens_x, "y", 4, 1)
    tokens_across = shift(tokens_x, "y", 4, 2)
    cot_y, _ = barrier((cot_y, far_here))
    down = ring_gather(jnp.stack([down_own, down_far]))
    cot_own = [cot_y] + [shift(cot_y, X, 4, -d) for d in (1, 2, 3)]
    cot_own = jnp.stack(cot_own)
    tokens_own = jnp.stack([tokens_x, tokens_up, tokens_across, tokens_low])
    tokens_swap = shift(tokens_own, "c", 2, 1)
    cot_swap = shift(cot_own, "c", 2, 1)
    token_args = (tokens_own, tokens_swap, tokens_own, tokens_swap)
    cot_args = (cot_own, cot_swap, cot_own, cot_swap)

    def near_rows(s):
        return s, 0

    def far_rows(s):
        return s, 1

    rows_shape = (4, 2, RANGE, 512)
    (near_sums,) = call(
        near_sums_kernel,
        (4,),
        [by_z(2, 0)] + act_specs(near_rows, False),
        [(PAIR, F32)],
        [whole(PAIR)],
        [],
        FLOPS,
        (pos, near) + token_args,
    )
    sums, hidden = call(
        far_sums_kernel,
        (4,),
        [by_z(2, 0)] + act_specs(far_rows, False) + [whole(PAIR)],
        [(PAIR, F32), (SUMS, BF16)],
        [whole(PAIR), whole(SUMS)],
        [],
        FLOPS,
        (pos, far) + token_args + (near_sums,),
    )
    (down_rows,) = call(
        down_grads_kernel,
        (4,),
        [whole(SUMS)] + act_specs(near_rows, True) + act_specs(far_rows, True),
        [(rows_shape, BF16)],
        [by_z(2, 0)],
        [],
        FLOPS,
        (pos, hidden) + cot_args + cot_args,
    )
    down_rows, sums = barrier((down_rows, sums))
    down_sum = over_z_sum(down_rows)
    grads, turned = call(
        hidden_grad_kernel,
        (4,),
        [by_turned_z(1, 0), by_turned_z(1, 1)] + act_specs(near_rows, True) + act_specs(far_rows, True) + [whole(PAIR)],
        [(PAIR, BF16), (PAIR[::-1], BF16)],
        [whole(PAIR), whole(PAIR[::-1])],
        [pltpu.VMEM(SUMS, F32)],
        FLOPS,
        (pos, down, down) + cot_args + cot_args + (sums,),
    )

    def pair_rows(rows_of, out_spec, grads):
        return call(
            pair_grads_kernel,
            (4,),
            [whole(PAIR)] + act_specs(rows_of, False),
            [(rows_shape, BF16)],
            [out_spec],
            [],
            FLOPS,
            (pos, grads) + token_args,
        )[0]

    parts = token_grads(pos, turned, near, far)
    parts, grads = barrier((parts, grads))
    core_part = shift(parts[1], "c", 2, 1)
    far_grads = pair_rows(far_rows, by_z(2, 0), grads)
    far_sum = over_z_sum(far_grads)
    far_grads, grads = barrier((far_grads, grads))
    near_grads = pair_rows(near_rows, by_z(2, 0), grads)
    near_sum = over_z_sum(near_grads)
    of_chip = total_of((parts[0], core_part))
    y_blocks = send_four(of_chip, "y")
    down_back = shift(down_sum[1], "xl", 2, 1)
    far_row = far_sum * one
    far_back = shift(far_row, "xl", 2, 1)
    y_blocks, down_back = barrier((y_blocks, down_back))
    along_y = total_of(y_blocks)
    grad_tokens = total_of(send_four(along_y, X))
    grad_tokens, near_sum, far_back = barrier((grad_tokens, near_sum, far_back))
    gate_back, up_back = far_back[0], far_back[1]

    def own_rows(own, other, tile_keep):
        both = jnp.where(xl == 0, jnp.stack([own, other]), jnp.stack([other, own]))
        grad = both.reshape(2 * RANGE, 512).T
        return (grad.astype(F32) * expand(tile_keep).astype(F32)).astype(BF16)

    grad_down = own_rows(down_sum[0], down_back, down_keep)
    grad_gate = own_rows(near_sum[0], gate_back, gate_keep)
    grad_up = own_rows(near_sum[1], up_back, up_keep)
    return (grad_tokens, grad_gate, grad_up, grad_down)


def solution(mesh):
    fine = Mesh(mesh.devices.reshape(2, 4, 2, 4, 2), ("xl", "z", "xh", "y", "c"))
    spec = P(("xl", "z"), ("xh", "y", "c"))

    return jax.shard_map(
        on_device, mesh=fine, in_specs=(spec,) * 8, out_specs=(spec,) * 4, check_vma=False
    )
```

```python
import jax
import jax.numpy as jnp
from jax import lax
from jax.experimental import pallas as pl
from jax.experimental.pallas import tpu as pltpu
from jax.sharding import Mesh
from jax.sharding import PartitionSpec as P


F32 = jnp.float32
BF16 = jnp.bfloat16
X = ("xl", "xh")
VMEM_LIMIT = 56 * 1024 * 1024
NT = (((1,), (1,)), ((), ()))
NN = (((1,), (0,)), ((), ()))
RANGE = 448
TOKENS = 1024


def shift(value, axis, size, step):
    name = (lambda i: i % 2 * 2 + i // 2) if axis == X else (lambda i: i)
    return lax.ppermute(value, axis, [(name(i), name((i + step) % size)) for i in range(size)])


def expand(tile_keep):
    row_tiles, col_tiles = tile_keep.shape
    spread = jnp.broadcast_to(tile_keep[:, None, :, None], (row_tiles, 128, col_tiles, 128))
    return spread.reshape(row_tiles * 128, col_tiles * 128)


def gather_four(block, axis):
    return jnp.stack([block] + [shift(block, axis, 4, -d) for d in (1, 2, 3)])


def send_four(pieces, axis):
    return [pieces[0]] + [shift(pieces[d], axis, 4, d) for d in (1, 2, 3)]


def ring_gather(block):
    left, right = shift(block, "z", 4, 1), shift(block, "z", 4, -1)
    cut = (2, block.shape[0] * block.shape[1] // 2, block.shape[2])
    across = jnp.stack(
        [shift(left.reshape(cut)[0], "z", 4, 1), shift(right.reshape(cut)[1], "z", 4, -1)]
    )
    return jnp.stack([block, right, across.reshape(block.shape), left])


def total_of(blocks):
    return sum(b.astype(F32) for b in blocks).astype(BF16)


def turn_x(pos, xh, xl):
    return lax.rem(xh * 2 + xl + 4 - pos[0], 4)


def turn_y(pos, y):
    return lax.rem(y + 4 - pos[1], 4)


def act_specs(far_of, x_first):
    def spec(xl):
        def place(s, pos):
            z, far = far_of(s)
            turned = (turn_y(pos, z), turn_x(pos, far ^ pos[3], xl))
            return (turned[::-1] if x_first else turned) + (0, 0)

        return pl.BlockSpec((1, 1, 512, 256), place)

    return [spec(0), spec(0), spec(1), spec(1)]


def whole(shape):
    return pl.BlockSpec(shape, lambda *ids: (0,) * len(shape))


def by_z(count, first):
    return pl.BlockSpec((1, count, RANGE, 512), lambda s, *rest: (s, first, 0, 0))


def by_turned_z(count, first):
    def place(s, *rest):
        return (lax.rem(s + 4 - rest[-1][4], 4), first, 0, 0)

    return pl.BlockSpec((1, count, RANGE, 512), place)


def call(kernel, steps, in_specs, outs, out_specs, scratch, flops, args):
    moved = sum(a.size * a.dtype.itemsize for a in args)
    return pl.pallas_call(
        kernel,
        out_shape=[jax.ShapeDtypeStruct(shape, kind) for shape, kind in outs],
        grid_spec=pltpu.PrefetchScalarGridSpec(
            num_scalar_prefetch=1,
            grid=steps,
            in_specs=in_specs,
            out_specs=out_specs,
            scratch_shapes=scratch,
        ),
        compiler_params=pltpu.CompilerParams(vmem_limit_bytes=VMEM_LIMIT),
        cost_estimate=pl.CostEstimate(flops=flops, bytes_accessed=moved, transcendentals=0),
    )(*args)


FLOPS = 2 * RANGE * TOKENS * 4096
SUMS = (RANGE, TOKENS)
PAIR = (2 * RANGE, TOKENS)


def core_columns(pos):
    own = pl.ds(pl.multiple_of(pos[2] * 256, 256), 256)
    other = pl.ds(pl.multiple_of((1 - pos[2]) * 256, 256), 256)
    return own, other


def own_first(pos, w):
    own, other = core_columns(pos)
    return jnp.concatenate([w[:, own], w[:, other]], axis=1)


def beside(own_ref, other_ref):
    return jnp.concatenate([own_ref[0, 0], other_ref[0, 0]], axis=1)


HALVES = (slice(0, 512), slice(512, 1024))


def near_sums_kernel(pos, w_ref, a0, b0, a1, b1, sums_ref):
    first = pl.program_id(0) == 0
    w = own_first(pos, w_ref.at[0].reshape(2 * RANGE, 512))
    for cols, (own, other) in zip(HALVES, ((a0, b0), (a1, b1))):
        term = lax.dot_general(w, beside(own, other), NT, preferred_element_type=F32)

        @pl.when(first)
        def _():
            sums_ref[:, cols] = term

        @pl.when(jnp.logical_not(first))
        def _():
            sums_ref[:, cols] += term


def far_sums_kernel(pos, w_ref, a0, b0, a1, b1, near_ref, sums_ref, hidden_ref):
    first = pl.program_id(0) == 0
    w = own_first(pos, w_ref.at[0].reshape(2 * RANGE, 512))
    for cols, (own, other) in zip(HALVES, ((a0, b0), (a1, b1))):
        term = lax.dot_general(w, beside(own, other), NT, preferred_element_type=F32)

        @pl.when(first)
        def _():
            sums_ref[:, cols] = near_ref[:, cols] + term

        @pl.when(jnp.logical_not(first))
        def _():
            sums_ref[:, cols] += term

    @pl.when(pl.program_id(0) == 3)
    def _():
        @pl.loop(0, RANGE // 16)
        def _(i):
            gate = sums_ref[pl.ds(i * 16, 16), :]
            up = sums_ref[pl.ds(RANGE + i * 16, 16), :]
            hidden_ref[pl.ds(i * 16, 16), :] = (gate * jax.nn.sigmoid(gate) * up).astype(BF16)


def hidden_grad_kernel(
    pos, near_ref, far_ref, a0, b0, a1, b1, c0, d0, c1, d1, sums_ref, grads_ref, turned_ref, acc
):
    first = pl.program_id(0) == 0
    near, far = own_first(pos, near_ref.at[0, 0]), own_first(pos, far_ref.at[0, 0])
    for cols, pairs in zip(HALVES, ((a0, b0, c0, d0), (a1, b1, c1, d1))):
        term = lax.dot_general(near, beside(*pairs[:2]), NT, preferred_element_type=F32)
        term += lax.dot_general(far, beside(*pairs[2:]), NT, preferred_element_type=F32)

        @pl.when(first)
        def _():
            acc[:, cols] = term

        @pl.when(jnp.logical_not(first))
        def _():
            acc[:, cols] += term

    @pl.when(pl.program_id(0) == 3)
    def _():
        @pl.loop(0, RANGE // 16)
        def _(i):
            gates, ups = pl.ds(i * 16, 16), pl.ds(RANGE + i * 16, 16)
            gate, up, grad = sums_ref[gates, :], sums_ref[ups, :], acc[gates, :]
            sig = jax.nn.sigmoid(gate)
            grads_ref[gates, :] = (grad * up * sig * (1.0 + gate * (1.0 - sig))).astype(BF16)
            grads_ref[ups, :] = (grad * gate * sig).astype(BF16)

        @pl.loop(0, TOKENS // 128)
        def _(i):
            part = pl.ds(pl.multiple_of(i * 128, 128), 128)
            turned_ref[part, :] = grads_ref[:, part].T


def pair_grads_kernel(pos, g_ref, a0, b0, a1, b1, out_ref):
    own, other = core_columns(pos)
    for cols, low, high in ((own, a0, a1), (other, b0, b1)):
        acts = jnp.concatenate([low[0, 0], high[0, 0]], axis=0)
        term = lax.dot_general(g_ref[...], acts, NN, preferred_element_type=F32).astype(BF16)
        out_ref[0, 0, :, cols] = term[:RANGE]
        out_ref[0, 1, :, cols] = term[RANGE:]


def down_grads_kernel(pos, h_ref, a0, b0, a1, b1, c0, d0, c1, d1, out_ref):
    own, other = core_columns(pos)
    for place, cols, low, high in ((0, own, a0, a1), (0, other, b0, b1), (1, own, c0, c1), (1, other, d0, d1)):
        acts = jnp.concatenate([low[0, 0], high[0, 0]], axis=0)
        term = lax.dot_general(h_ref[...], acts, NN, preferred_element_type=F32)
        out_ref[0, place, :, cols] = term.astype(BF16)


def token_grads_kernel(pos, g_ref, near_ref, far_ref, own_ref, other_ref):
    here, far = pos[2], pl.program_id(1)
    near_w, far_w = (ref.at[0].reshape(2 * RANGE, 512)[...] for ref in (near_ref, far_ref))
    w = jnp.where(far == 0, near_w, far_w)
    term = lax.dot_general(g_ref[...], w, NN, preferred_element_type=F32).astype(BF16)
    low, high = term[:, :256], term[:, 256:]
    own, other = jnp.where(here == 0, low, high), jnp.where(here == 0, high, low)
    for xl in (0, 1):
        place = turn_x(pos, far ^ pos[3], xl)
        own_ref[0, place] = own[xl * 512 : (xl + 1) * 512]
        other_ref[0, place] = other[xl * 512 : (xl + 1) * 512]


def token_grads(pos, turned, near, far_w):
    def place(z, far, pos):
        return (turn_y(pos, z), 0, 0, 0)

    return call(
        token_grads_kernel,
        (4, 2),
        [whole(turned.shape), by_z(2, 0), by_z(2, 0)],
        [((4, 4, 512, 256), BF16)] * 2,
        [pl.BlockSpec((1, 4, 512, 256), place)] * 2,
        [],
        2 * FLOPS,
        (pos, turned, near, far_w),
    )


def on_device(
    tokens, cotangent, gate_weight, up_weight, down_weight, gate_keep, up_keep, down_keep
):
    xl = lax.axis_index("xl")
    place_x = lax.axis_index("xh") * 2 + xl
    pos = jnp.stack(
        [place_x, lax.axis_index("y"), lax.axis_index("c"), xl, lax.axis_index("z")]
    ).astype(jnp.int32)
    barrier = lax.optimization_barrier
    one = (pos[4] < 4).astype(BF16)

    def ranges(weight, tile_keep):
        kept = (weight * expand(tile_keep).astype(BF16)).T.reshape(2, RANGE, 512)
        return (
            lax.dynamic_index_in_dim(kept, xl, 0, keepdims=False),
            lax.dynamic_index_in_dim(kept, 1 - xl, 0, keepdims=False),
        )

    gate_own, gate_other = ranges(gate_weight, gate_keep)
    up_own, up_other = ranges(up_weight, up_keep)
    down_own, down_other = ranges(down_weight, down_keep)

    def over_z_sum(rows):
        return lax.psum_scatter(rows, "z", scatter_dimension=0, tiled=True)[0]

    def over_z(rows):
        return lax.all_gather(rows[None], "z", axis=0, tiled=True)

    near = over_z(jnp.stack([gate_own, up_own]))
    tokens_x = gather_four(tokens, X)
    cot_y = gather_four(cotangent, "y")
    tokens_x, cot_y, gate_other, up_other, down_other = barrier(
        (tokens_x, cot_y, gate_other, up_other, down_other)
    )
    gate_far, up_far = shift(gate_other, "xl", 2, 1), shift(up_other, "xl", 2, 1)
    down_far = shift(down_other, "xl", 2, 1)
    far_here = jnp.stack([gate_far, up_far])
    far = over_z(far_here)
    tokens_up, tokens_low = shift(tokens_x, "y", 4, -1), shift(tokens_x, "y", 4, 1)
    tokens_across = shift(tokens_x, "y", 4, 2)
    cot_y, _ = barrier((cot_y, far_here))
    down = ring_gather(jnp.stack([down_own, down_far]))
    cot_own = [cot_y] + [shift(cot_y, X, 4, -d) for d in (1, 2, 3)]
    cot_own = jnp.stack(cot_own)
    tokens_own = jnp.stack([tokens_x, tokens_up, tokens_across, tokens_low])
    tokens_swap = shift(tokens_own, "c", 2, 1)
    cot_swap = shift(cot_own, "c", 2, 1)
    token_args = (tokens_own, tokens_swap, tokens_own, tokens_swap)
    cot_args = (cot_own, cot_swap, cot_own, cot_swap)

    def near_rows(s):
        return s, 0

    def far_rows(s):
        return s, 1

    rows_shape = (4, 2, RANGE, 512)
    (near_sums,) = call(
        near_sums_kernel,
        (4,),
        [by_z(2, 0)] + act_specs(near_rows, False),
        [(PAIR, F32)],
        [whole(PAIR)],
        [],
        FLOPS,
        (pos, near) + token_args,
    )
    sums, hidden = call(
        far_sums_kernel,
        (4,),
        [by_z(2, 0)] + act_specs(far_rows, False) + [whole(PAIR)],
        [(PAIR, F32), (SUMS, BF16)],
        [whole(PAIR), whole(SUMS)],
        [],
        FLOPS,
        (pos, far) + token_args + (near_sums,),
    )
    (down_rows,) = call(
        down_grads_kernel,
        (4,),
        [whole(SUMS)] + act_specs(near_rows, True) + act_specs(far_rows, True),
        [(rows_shape, BF16)],
        [by_z(2, 0)],
        [],
        FLOPS,
        (pos, hidden) + cot_args + cot_args,
    )
    down_rows, sums = barrier((down_rows, sums))
    down_sum = over_z_sum(down_rows)
    grads, turned = call(
        hidden_grad_kernel,
        (4,),
        [by_turned_z(1, 0), by_turned_z(1, 1)] + act_specs(near_rows, True) + act_specs(far_rows, True) + [whole(PAIR)],
        [(PAIR, BF16), (PAIR[::-1], BF16)],
        [whole(PAIR), whole(PAIR[::-1])],
        [pltpu.VMEM(SUMS, F32)],
        FLOPS,
        (pos, down, down) + cot_args + cot_args + (sums,),
    )

    def pair_rows(rows_of, out_spec, grads):
        return call(
            pair_grads_kernel,
            (4,),
            [whole(PAIR)] + act_specs(rows_of, False),
            [(rows_shape, BF16)],
            [out_spec],
            [],
            FLOPS,
            (pos, grads) + token_args,
        )[0]

    parts = token_grads(pos, turned, near, far)
    parts, grads = barrier((parts, grads))
    core_part = shift(parts[1], "c", 2, 1)
    far_grads = pair_rows(far_rows, by_z(2, 0), grads)
    far_sum = over_z_sum(far_grads)
    far_grads, grads = barrier((far_grads, grads))
    near_grads = pair_rows(near_rows, by_z(2, 0), grads)
    near_sum = over_z_sum(near_grads)
    of_chip = total_of((parts[0], core_part))
    y_blocks = send_four(of_chip, "y")
    down_back = shift(down_sum[1], "xl", 2, 1)
    far_row = far_sum * one
    far_back = shift(far_row, "xl", 2, 1)
    y_blocks, down_back = barrier((y_blocks, down_back))
    along_y = total_of(y_blocks)
    grad_tokens = total_of(send_four(along_y, X))
    grad_tokens, near_sum, far_back = barrier((grad_tokens, near_sum, far_back))
    gate_back, up_back = far_back[0], far_back[1]

    def own_rows(own, other, tile_keep):
        both = jnp.where(xl == 0, jnp.stack([own, other]), jnp.stack([other, own]))
        grad = both.reshape(2 * RANGE, 512).T
        return (grad.astype(F32) * expand(tile_keep).astype(F32)).astype(BF16)

    grad_down = own_rows(down_sum[0], down_back, down_keep)
    grad_gate = own_rows(near_sum[0], gate_back, gate_keep)
    grad_up = own_rows(near_sum[1], up_back, up_keep)
    return (grad_tokens, grad_gate, grad_up, grad_down)


def solution(mesh):
    fine = Mesh(mesh.devices.reshape(2, 4, 2, 4, 2), ("xl", "z", "xh", "y", "c"))
    spec = P(("xl", "z"), ("xh", "y", "c"))

    return jax.shard_map(
        on_device, mesh=fine, in_specs=(spec,) * 8, out_specs=(spec,) * 4, check_vma=False
    )
```
